32 devices in a mesh: freq: 4 (over y, x), tile: 8 (over z, core).
Axes of the slice: x: 2, y: 2, z: 4, core: 2. Of those that a mesh axis runs over, the one named last changes fastest.
Arguments:
- voltages: bfloat16 [4096, 24960], P(('freq', 'tile')), may hold values from -16 to 16, as said below
- channel_ids: int32 [12], replicated, may hold values from 1 to 63
- start_basis: float32 [2, 8, 4096], replicated, may hold values from -0.0625 to 0.0625
Outputs:
- cleaned: float32 [2, 12, 192, 4096], P(None, 'freq', 'tile')
The draws below stay inside these ranges and needn't reach their ends.
Inputs may be any that keep to these rules, and one draw needn't show every extreme that they name: `voltages`: real samples of each input over the whole window.
All inputs are finite; a program needn't handle non-finite values.
Results may differ from the reference program's by a relative error of at most 0.0048.
Values may be sent and summed in bfloat16 or wider, within the bound.
A program may use at most 128 MiB of HBM per device.

```python
import math
import jax
import jax.numpy as jnp
from jax import lax

INPUTS = 4096
TAPS = 4
P_SIZE = 128
KDIM = 8
ITERS = 3
CHANNELS = 12
SPECTRA = 192
SAMPLES = 24960


highest = lax.Precision.HIGHEST


def draw_voltages(key, part):
    key_gain = jax.random.fold_in(key, 11)
    key_signal = jax.random.fold_in(key, 12)
    key_power = jax.random.fold_in(key, 13)
    key_noise = jax.random.fold_in(key, 14)
    sources = KDIM + 2
    powers = jnp.exp(jax.random.uniform(key_power, (sources,), jnp.float32, math.log(0.001), math.log(0.2)))
    time_frac = jnp.arange(SAMPLES, dtype=jnp.float32) / SAMPLES
    envelope = 0.6 + 1.2 * time_frac
    signals = jax.random.normal(key_signal, (sources, SAMPLES), jnp.float32) * jnp.sqrt(powers)[:, None] * envelope[None, :]
    gain_table = jax.random.normal(key_gain, (INPUTS, sources), jnp.float32)
    block_rows = min(INPUTS, 128)
    block_count = INPUTS // block_rows

    def one_block(block_at):
        first_row = block_at * block_rows
        gain_rows = lax.dynamic_slice_in_dim(gain_table, first_row, block_rows, 0)
        fraction = (first_row + jnp.arange(block_rows, dtype=jnp.int32)).astype(jnp.float32) / INPUTS
        noise_key = jax.random.fold_in(key_noise, block_at)
        noise_draw = jax.random.normal(noise_key, (block_rows, SAMPLES), jnp.float32)
        amplitude = 0.5 + fraction
        combined = amplitude[:, None] * (noise_draw + jnp.dot(gain_rows, signals, precision=highest))
        return jnp.clip(combined, -16.0, 16.0).astype(jnp.bfloat16)
    blocks = lax.map(one_block, jnp.arange(block_count, dtype=jnp.int32))
    return blocks.reshape(INPUTS, SAMPLES)


def place_ends(drawn, rng, low, top_value):
    longest = drawn.shape.index(max(drawn.shape))
    spots = []
    for shift in (0, 1):
        where = [jax.random.randint(jax.random.fold_in(rng, axis), (), 0, length) for axis, length in enumerate(drawn.shape)]
        where[longest] = (where[longest] + shift) % drawn.shape[longest]
        spots.append(tuple(where))
    return drawn.at[spots[0]].set(low).at[spots[1]].set(top_value)


def centred(rng, shape, spread, limit, kind=jnp.bfloat16):
    values = jax.random.normal(rng, shape, jnp.float32) * spread
    return jnp.minimum(jnp.maximum(values, -limit), limit).astype(kind)


def setup_inputs(seed: int = 0) -> dict:
    seeds = jax.random.split(jax.random.key(seed), 4)
    voltages = draw_voltages(jax.random.fold_in(seeds[3], 71), 0)
    channel_ids = place_ends(jax.random.randint(seeds[1], (CHANNELS,), 1, P_SIZE // 2), jax.random.fold_in(seeds[1], 1), 1, (P_SIZE // 2) - 1).astype(jnp.int32)
    start_basis = centred(seeds[2], (2, KDIM, INPUTS), (2 * INPUTS) ** -0.5, 0.0625, jnp.float32)
    return dict(voltages=voltages, channel_ids=channel_ids, start_basis=start_basis)


loading = 0.5
highest = lax.Precision.HIGHEST

def make_table(channel_ids, taps_count, points):
    length = taps_count * points
    offsets = jnp.arange(length, dtype=jnp.float32)
    shifted = (offsets + 0.5 - length / 2.0) / points
    window = jnp.sinc(shifted) * (0.5 - 0.5 * jnp.cos(2.0 * math.pi * (offsets + 0.5) / length))
    window = window / jnp.sqrt(jnp.sum(window * window))
    window = window.reshape(taps_count, points)
    phases = channel_ids[:, None] * jnp.arange(points, dtype=jnp.int32)[None, :] % points
    angles = 2.0 * math.pi / points * phases.astype(jnp.float32)
    rotors = jnp.stack([jnp.cos(angles), -jnp.sin(angles)])
    return (window[:, None, None, :] * rotors[None]).astype(jnp.bfloat16)

def channelize(voltages, coeffs):
    block_rows = min(INPUTS, 128)
    block_count = INPUTS // block_rows
    filter_table = coeffs.astype(jnp.float32)

    def one_block(first_row):
        chosen = lax.dynamic_slice_in_dim(voltages, first_row, block_rows, 0)
        frames = chosen.reshape(block_rows, SPECTRA + TAPS - 1, P_SIZE).astype(jnp.float32)
        summed = jnp.zeros((2, CHANNELS, SPECTRA, block_rows), jnp.float32)
        for offset in range(TAPS):
            summed = summed + jnp.einsum('rcp,isp->rcsi', filter_table[offset], frames[:, offset:offset + SPECTRA, :], precision=highest)
        return summed.astype(jnp.bfloat16)
    starts = (jnp.arange(block_count) * block_rows).astype(jnp.int32)
    stacked = lax.map(one_block, starts)
    return jnp.transpose(stacked, (1, 2, 3, 0, 4)).reshape(2, CHANNELS, SPECTRA, INPUTS)

def contract(form, left, right):
    return jnp.einsum(form, left, right, precision=highest)

def image_of(values, basis):
    real_v, imag_v = (values[0], values[1])
    real_q, imag_q = (basis[0], basis[1])
    weight_re = contract('csi,cki->csk', real_v, real_q) + contract('csi,cki->csk', imag_v, imag_q)
    weight_im = contract('csi,cki->csk', real_v, imag_q) - contract('csi,cki->csk', imag_v, real_q)
    image_re = contract('csi,csk->cki', real_v, weight_re) - contract('csi,csk->cki', imag_v, weight_im)
    image_im = contract('csi,csk->cki', real_v, weight_im) + contract('csi,csk->cki', imag_v, weight_re)
    return jnp.stack([image_re, image_im])

def gram_parts(image):
    real_z, imag_z = (image[0], image[1])
    gram_re = contract('cki,cji->ckj', real_z, real_z) + contract('cki,cji->ckj', imag_z, imag_z)
    gram_im = contract('cki,cji->ckj', real_z, imag_z) - contract('cki,cji->ckj', imag_z, real_z)
    return (gram_re, gram_im)

def lower_factor(gram_re, gram_im):
    basis_width = gram_re.shape[-1]
    lower_re = {}
    lower_im = {}
    pivots = []
    for column in range(basis_width):
        pivot_square = gram_re[:, column, column]
        for earlier in range(column):
            pivot_square = pivot_square - lower_re[column, earlier] ** 2 - lower_im[column, earlier] ** 2
        pivot_value = jnp.sqrt(pivot_square)
        pivots.append(pivot_value)
        for row_at in range(column + 1, basis_width):
            value_re = gram_re[:, row_at, column]
            value_im = gram_im[:, row_at, column]
            for earlier in range(column):
                left_re, left_im = (lower_re[row_at, earlier], lower_im[row_at, earlier])
                right_re, right_im = (lower_re[column, earlier], lower_im[column, earlier])
                value_re = value_re - (left_re * right_re + left_im * right_im)
                value_im = value_im - (left_im * right_re - left_re * right_im)
            lower_re[row_at, column] = value_re / pivot_value
            lower_im[row_at, column] = value_im / pivot_value
    return (lower_re, lower_im, pivots)

def apply_factor(image, lower_re, lower_im, pivots):
    basis_width = image.shape[2]
    result_re = []
    result_im = []
    for column in range(basis_width):
        value_re = image[0, :, column, :]
        value_im = image[1, :, column, :]
        for earlier in range(column):
            left_re, left_im = (result_re[earlier], result_im[earlier])
            right_re = lower_re[column, earlier][:, None]
            right_im = lower_im[column, earlier][:, None]
            value_re = value_re - (left_re * right_re + left_im * right_im)
            value_im = value_im - (left_im * right_re - left_re * right_im)
        divisor = pivots[column][:, None]
        result_re.append(value_re / divisor)
        result_im.append(value_im / divisor)
    return jnp.stack([jnp.stack(result_re, axis=1), jnp.stack(result_im, axis=1)])

def remove_subspace(values, basis):
    real_v, imag_v = (values[0], values[1])
    real_q, imag_q = (basis[0], basis[1])
    coord_re = contract('cki,csi->cks', real_q, real_v) + contract('cki,csi->cks', imag_q, imag_v)
    coord_im = contract('cki,csi->cks', real_q, imag_v) - contract('cki,csi->cks', imag_q, real_v)
    fitted_re = contract('cki,cks->csi', real_q, coord_re) - contract('cki,cks->csi', imag_q, coord_im)
    fitted_im = contract('cki,cks->csi', real_q, coord_im) + contract('cki,cks->csi', imag_q, coord_re)
    return values - jnp.stack([fitted_re, fitted_im])

def reference(voltages, channel_ids, start_basis):
    coeffs = make_table(channel_ids, TAPS, P_SIZE)
    spectra = channelize(voltages, coeffs)
    values = spectra.astype(jnp.float32)
    basis = jnp.broadcast_to(start_basis[:, None], (2, CHANNELS, KDIM, INPUTS))
    for step_at in range(ITERS):
        image = image_of(values, basis) / SPECTRA + loading * basis
        gram_re, gram_im = gram_parts(image)
        lower_re, lower_im, pivots = lower_factor(gram_re, gram_im)
        basis = apply_factor(image, lower_re, lower_im, pivots)
    return remove_subspace(values, basis)
```

```python
import functools
import math

import jax
import jax.numpy as jnp
from jax import lax
from jax.experimental import pallas as pl
from jax.experimental.pallas import tpu as pltpu
from jax.sharding import PartitionSpec as P

TAPS = 4
P_SIZE = 128
ITERS = 3
STEP = 16

loading = 0.5
highest = lax.Precision.HIGHEST
VMEM = pl.BlockSpec(memory_space=pltpu.VMEM)
MESH = pl.DeviceIdType.MESH


def make_table(channel_ids, taps_count, points):
    length = taps_count * points
    offsets = jnp.arange(length, dtype=jnp.float32)
    shifted = (offsets + 0.5 - length / 2.0) / points
    window = jnp.sinc(shifted) * (0.5 - 0.5 * jnp.cos(2.0 * math.pi * (offsets + 0.5) / length))
    window = window / jnp.sqrt(jnp.sum(window * window))
    window = window.reshape(taps_count, points)
    phases = channel_ids[:, None] * jnp.arange(points, dtype=jnp.int32)[None, :] % points
    angles = 2.0 * math.pi / points * phases.astype(jnp.float32)
    rotors = jnp.stack([jnp.cos(angles), -jnp.sin(angles)])
    return (window[:, None, None, :] * rotors[None]).astype(jnp.bfloat16)


def banded(coeffs):
    rows = coeffs.shape[1]
    spect = lax.broadcasted_iota(jnp.int32, (1, STEP, STEP + TAPS - 1, 1), 1)
    frame = lax.broadcasted_iota(jnp.int32, (1, STEP, STEP + TAPS - 1, 1), 2)
    table = jnp.zeros((rows, STEP, STEP + TAPS - 1, P_SIZE), jnp.bfloat16)
    for tap in range(TAPS):
        table = jnp.where(frame - spect == tap, coeffs[tap][:, None, None, :], table)
    return table.reshape(rows * STEP, (STEP + TAPS - 1) * P_SIZE)


def nt(left, right):
    return lax.dot_general(left, right, (((1,), (1,)), ((), ())), preferred_element_type=jnp.float32)


def channelize_kernel(volts_ref, table_ref, out_ref):
    step = pl.program_id(0)
    span = (STEP + TAPS - 1) * P_SIZE
    start = pl.multiple_of(step * (STEP * P_SIZE), P_SIZE)
    chunk = volts_ref[:, pl.ds(start, span)]
    result = nt(table_ref[...], chunk)
    out_ref[...] = result.reshape(out_ref.shape).astype(jnp.bfloat16)


def channelize(voltages, table, rows, spectra_all):
    inputs_local, samples = voltages.shape
    return pl.pallas_call(
        channelize_kernel,
        grid=(spectra_all // STEP,),
        in_specs=[VMEM, VMEM],
        out_specs=pl.BlockSpec((rows, STEP, inputs_local), lambda i: (0, i, 0)),
        out_shape=jax.ShapeDtypeStruct((rows, spectra_all, inputs_local), jnp.bfloat16),
        compiler_params=pltpu.CompilerParams(vmem_limit_bytes=40 * 2**20),
    )(voltages, table)


def split3(value):
    high = value.astype(jnp.bfloat16)
    rest = value - high.astype(jnp.float32)
    mid = rest.astype(jnp.bfloat16)
    low = (rest - mid.astype(jnp.float32)).astype(jnp.bfloat16)
    return jnp.concatenate([high, mid, low], axis=0)


def fold3(value):
    rows = value.shape[0] // 3
    return value[:rows] + value[rows : 2 * rows] + value[2 * rows :]


def plain(left, right):
    return lax.dot_general(left, right, (((1,), (0,)), ((), ())), preferred_element_type=jnp.float32)


def project(z, real_v, imag_v, k):
    parts = split3(z)
    on_re = fold3(nt(parts, real_v))
    on_im = fold3(nt(parts, imag_v))
    return jnp.concatenate([on_re[:k] + on_im[k:], on_re[k:] - on_im[:k]], axis=0)


def inverse_factor(gram, k):
    lanes = gram.shape[1]
    col = lax.broadcasted_iota(jnp.int32, (k, lanes), 1)
    row = lax.broadcasted_iota(jnp.int32, (k, lanes), 0)
    zero = jnp.zeros((k, lanes), jnp.float32)
    a_re = gram[:k]
    a_im = gram[k:]
    m_re = jnp.where(col == row, 1.0, zero)
    m_im = zero
    for j in range(k):
        at_col = col == j
        c_re = jnp.sum(jnp.where(at_col, a_re, 0.0), axis=1, keepdims=True)
        c_im = jnp.sum(jnp.where(at_col, a_im, 0.0), axis=1, keepdims=True)
        pivot = jnp.sqrt(c_re[j : j + 1])
        l_re = jnp.where(row[:, :1] > j, c_re / pivot, 0.0)
        l_im = jnp.where(row[:, :1] > j, c_im / pivot, 0.0)
        ar, ai = a_re[j : j + 1] / pivot, a_im[j : j + 1] / pivot
        mr, mi = m_re[j : j + 1] / pivot, m_im[j : j + 1] / pivot
        here = row == j
        a_re = jnp.where(here, ar, a_re - (l_re * ar - l_im * ai))
        a_im = jnp.where(here, ai, a_im - (l_re * ai + l_im * ar))
        m_re = jnp.where(here, mr, m_re - (l_re * mr - l_im * mi))
        m_im = jnp.where(here, mi, m_im - (l_re * mi + l_im * mr))
    return m_re, -m_im


def mix(m_re, m_im, rows, k):
    out_re = jnp.zeros((k, rows.shape[1]), jnp.float32)
    out_im = jnp.zeros((k, rows.shape[1]), jnp.float32)
    for j in range(k):
        f_re, f_im = m_re[:, j : j + 1], m_im[:, j : j + 1]
        r_re, r_im = rows[j : j + 1], rows[k + j : k + j + 1]
        out_re = out_re + (f_re * r_re - f_im * r_im)
        out_im = out_im + (f_re * r_im + f_im * r_re)
    return jnp.concatenate([out_re, out_im], axis=0)


def start_kernel(v_ref, q_ref, pg_ref, *, k, lanes):
    chans, _, spectra, _ = v_ref.shape
    pg_ref[...] = jnp.zeros_like(pg_ref)
    for c in range(chans):
        pg_ref[2 * k * c : 2 * k * (c + 1), :spectra] = project(q_ref[...], v_ref[c, 0], v_ref[c, 1], k)


def step_kernel(v_ref, z_ref, pg_ref, z_out, pg_out, *, k, lanes, first):
    chans, _, spectra, width = v_ref.shape
    pg_out[...] = jnp.zeros_like(pg_out)
    for c in range(chans):
        at = slice(2 * k * c, 2 * k * (c + 1))
        weights = pg_ref[at, :spectra]
        basis = z_ref[...] if first else z_ref[c]
        if not first:
            m_re, m_im = inverse_factor(pg_ref[at, lanes:], k)
            weights = mix(m_re, m_im, weights, k)
            basis = mix(m_re, m_im, basis, k)
        real_v, imag_v = v_ref[c, 0], v_ref[c, 1]
        parts = split3(weights / spectra)
        on_re = fold3(plain(parts, real_v))
        on_im = fold3(plain(parts, imag_v))
        z = jnp.concatenate([on_re[:k] - on_im[k:], on_re[k:] + on_im[:k]], axis=0) + loading * basis
        z_out[c] = z
        pg_out[at, :spectra] = project(z, real_v, imag_v, k)
        pad = jnp.zeros((lanes_pad(k), width), jnp.float32)
        right = jnp.concatenate([z[:k], pad], axis=0)
        right_im = jnp.concatenate([z[k:], pad], axis=0)
        dims = (((1,), (1,)), ((), ()))
        first_dot = lax.dot_general(z, right, dims, precision=highest, preferred_element_type=jnp.float32)
        second_dot = lax.dot_general(z, right_im, dims, precision=highest, preferred_element_type=jnp.float32)
        g_re = first_dot[:k] + second_dot[k:]
        g_im = second_dot[:k] - first_dot[k:]
        pg_out[at, lanes:] = jnp.concatenate([g_re, g_im], axis=0)


def lanes_pad(k):
    return 128 - k


def tn(left, right):
    return lax.dot_general(left, right, (((0,), (0,)), ((), ())), preferred_element_type=jnp.float32)


def clean_kernel(v_ref, z_ref, pg_ref, out_ref, *, k, lanes):
    chans, _, spectra, width = v_ref.shape
    parts_count, _, _, block, _ = out_ref.shape
    for c in range(chans):
        at = slice(2 * k * c, 2 * k * (c + 1))
        m_re, m_im = inverse_factor(pg_ref[at, lanes:], k)
        w = mix(m_re, m_im, pg_ref[at, :spectra], k)
        q = mix(m_re, m_im, z_ref[c], k)
        turned = jnp.concatenate([q[k:], -q[:k]], axis=0)
        w3 = split3(w)
        n2 = 2 * k
        w_left = jnp.concatenate([w3[:n2], w3[:n2], w3[n2 : 2 * n2], w3[n2 : 2 * n2], w3[:n2], w3[2 * n2 :]], axis=0)
        for r, side in ((0, q), (1, turned)):
            s3 = split3(side)
            s_right = jnp.concatenate(
                [s3[:n2], s3[n2 : 2 * n2], s3[:n2], s3[n2 : 2 * n2], s3[2 * n2 :], s3[:n2]], axis=0
            )
            fitted = tn(w_left, s_right)
            cleaned = v_ref[c, r].astype(jnp.float32) - fitted
            out_ref[:, r, c] = cleaned.reshape(parts_count, block, width).astype(jnp.bfloat16)


def reduce_kernel(x_ref, out_ref, land_ref, send1, recv1, send2, recv2, *, size, chunk):
    me = lax.axis_index("tile")
    barrier = pltpu.get_barrier_semaphore()
    for d in range(1, size):
        peer = lax.rem(me + d, size)
        pl.semaphore_signal(barrier, inc=1, device_id={"tile": peer}, device_id_type=MESH)
    pl.semaphore_wait(barrier, size - 1)
    mine = pl.ds(pl.multiple_of(me * chunk, 8), chunk)
    sends = []
    for d in range(1, size):
        peer = lax.rem(me + d, size)
        copy = pltpu.make_async_remote_copy(
            src_ref=x_ref.at[pl.ds(pl.multiple_of(peer * chunk, 8), chunk)],
            dst_ref=land_ref.at[d - 1],
            send_sem=send1.at[d - 1],
            recv_sem=recv1.at[d - 1],
            device_id={"tile": peer},
            device_id_type=MESH,
        )
        copy.start()
        sends.append(copy)
    total = x_ref[mine]
    for d in range(1, size):
        sends[d - 1].wait_recv()
        total = total + land_ref[d - 1]
    out_ref[mine] = total
    later = []
    for d in range(1, size):
        peer = lax.rem(me + d, size)
        copy = pltpu.make_async_remote_copy(
            src_ref=out_ref.at[mine],
            dst_ref=out_ref.at[mine],
            send_sem=send2.at[d - 1],
            recv_sem=recv2.at[d - 1],
            device_id={"tile": peer},
            device_id_type=MESH,
        )
        copy.start()
        later.append(copy)
    for copy in later:
        copy.wait_recv()
    for copy in sends + later:
        copy.wait_send()


def tile_sum(x, size):
    rows, width = x.shape
    chunk = rows // size
    return pl.pallas_call(
        functools.partial(reduce_kernel, size=size, chunk=chunk),
        in_specs=[VMEM],
        out_specs=VMEM,
        out_shape=jax.ShapeDtypeStruct(x.shape, jnp.float32),
        scratch_shapes=[pltpu.VMEM((size - 1, chunk, width), jnp.float32)]
        + [pltpu.SemaphoreType.DMA((size - 1,))] * 4,
        compiler_params=pltpu.CompilerParams(collective_id=0, has_side_effects=True),
    )(x)


def up(value, unit):
    return -(-value // unit) * unit


def body(voltages, channel_ids, start_basis):
    inputs_local, samples_count = voltages.shape
    freq_count = lax.axis_size("freq")
    tile_count = lax.axis_size("tile")
    channels = channel_ids.shape[0]
    chan_local = channels // freq_count
    spectra_all = samples_count // P_SIZE - TAPS + 1
    spectra_local = spectra_all // tile_count
    k = start_basis.shape[1]
    width = freq_count * inputs_local

    coeffs = make_table(channel_ids, TAPS, P_SIZE).reshape(TAPS, 2 * channels, P_SIZE)
    local = channelize(voltages, banded(coeffs), 2 * channels, spectra_all)
    parcel = local.reshape(2, freq_count, chan_local, spectra_all, inputs_local)
    arrived = lax.all_to_all(parcel, "freq", split_axis=1, concat_axis=1, tiled=True)
    values = jnp.transpose(arrived, (2, 0, 3, 1, 4)).reshape(chan_local, 2, spectra_all, width)

    mine = lax.axis_index("tile")
    start = start_basis.reshape(2 * k, freq_count, tile_count, inputs_local)
    start = lax.dynamic_index_in_dim(start, mine, 2, keepdims=False).reshape(2 * k, width)

    lanes = up(spectra_all, 128)
    chunk = up(-(-chan_local * 2 * k // tile_count), 8)
    packed = jax.ShapeDtypeStruct((tile_count * chunk, lanes + 128), jnp.float32)
    z_shape = jax.ShapeDtypeStruct((chan_local, 2 * k, width), jnp.float32)
    params = pltpu.CompilerParams(vmem_limit_bytes=40 * 2**20)

    partial = pl.pallas_call(
        functools.partial(start_kernel, k=k, lanes=lanes),
        in_specs=[VMEM] * 2, out_specs=VMEM, out_shape=packed, compiler_params=params,
    )(values, start)
    z = start
    for step_at in range(ITERS):
        total = tile_sum(partial, tile_count)
        z, partial = pl.pallas_call(
            functools.partial(step_kernel, k=k, lanes=lanes, first=step_at == 0),
            in_specs=[VMEM] * 3, out_specs=[VMEM] * 2, out_shape=[z_shape, packed],
            compiler_params=params,
        )(values, z, total)
    total = tile_sum(partial, tile_count)
    cleaned = pl.pallas_call(
        functools.partial(clean_kernel, k=k, lanes=lanes),
        in_specs=[VMEM] * 3, out_specs=VMEM,
        out_shape=jax.ShapeDtypeStruct((tile_count, 2, chan_local, spectra_local, width), jnp.bfloat16),
        compiler_params=params,
    )(values, z, total)
    moved = lax.all_to_all(cleaned, "tile", split_axis=0, concat_axis=0, tiled=True)
    moved = moved.reshape(tile_count, 2, chan_local, spectra_local, freq_count, inputs_local)
    moved = jnp.transpose(moved, (1, 2, 3, 4, 0, 5)).astype(jnp.float32)
    return moved.reshape(2, chan_local, spectra_local, freq_count * tile_count * inputs_local)


def solution(mesh):
    in_specs = (P(("freq", "tile"), None), P(), P())
    out_specs = P(None, "freq", "tile", None)
    return jax.shard_map(body, mesh=mesh, in_specs=in_specs, out_specs=out_specs, check_vma=False)
```

```python
import functools
import math

import jax
import jax.numpy as jnp
from jax import lax
from jax.experimental import pallas as pl
from jax.experimental.pallas import tpu as pltpu
from jax.sharding import PartitionSpec as P

TAPS = 4
P_SIZE = 128
ITERS = 3
STEP = 16

loading = 0.5
highest = lax.Precision.HIGHEST
VMEM = pl.BlockSpec(memory_space=pltpu.VMEM)
MESH = pl.DeviceIdType.MESH


def make_table(channel_ids, taps_count, points):
    length = taps_count * points
    offsets = jnp.arange(length, dtype=jnp.float32)
    shifted = (offsets + 0.5 - length / 2.0) / points
    window = jnp.sinc(shifted) * (0.5 - 0.5 * jnp.cos(2.0 * math.pi * (offsets + 0.5) / length))
    window = window / jnp.sqrt(jnp.sum(window * window))
    window = window.reshape(taps_count, points)
    phases = channel_ids[:, None] * jnp.arange(points, dtype=jnp.int32)[None, :] % points
    angles = 2.0 * math.pi / points * phases.astype(jnp.float32)
    rotors = jnp.stack([jnp.cos(angles), -jnp.sin(angles)])
    return (window[:, None, None, :] * rotors[None]).astype(jnp.bfloat16)


def banded(coeffs):
    rows = coeffs.shape[1]
    spect = lax.broadcasted_iota(jnp.int32, (1, STEP, STEP + TAPS - 1, 1), 1)
    frame = lax.broadcasted_iota(jnp.int32, (1, STEP, STEP + TAPS - 1, 1), 2)
    table = jnp.zeros((rows, STEP, STEP + TAPS - 1, P_SIZE), jnp.bfloat16)
    for tap in range(TAPS):
        table = jnp.where(frame - spect == tap, coeffs[tap][:, None, None, :], table)
    return table.reshape(rows * STEP, (STEP + TAPS - 1) * P_SIZE)


def nt(left, right):
    return lax.dot_general(left, right, (((1,), (1,)), ((), ())), preferred_element_type=jnp.float32)


def split3(value):
    high = value.astype(jnp.bfloat16)
    rest = value - high.astype(jnp.float32)
    mid = rest.astype(jnp.bfloat16)
    low = (rest - mid.astype(jnp.float32)).astype(jnp.bfloat16)
    return jnp.concatenate([high, mid, low], axis=0)


def fold3(value):
    rows = value.shape[0] // 3
    return value[:rows] + value[rows : 2 * rows] + value[2 * rows :]


def plain(left, right):
    return lax.dot_general(left, right, (((1,), (0,)), ((), ())), preferred_element_type=jnp.float32)


def project(z, real_v, imag_v, k):
    parts = split3(z)
    on_re = fold3(nt(parts, real_v))
    on_im = fold3(nt(parts, imag_v))
    return jnp.concatenate([on_re[:k] + on_im[k:], on_re[k:] - on_im[:k]], axis=0)


def inverse_factor(gram, k, off=0):
    lanes = gram.shape[1]
    col = lax.broadcasted_iota(jnp.int32, (k, lanes), 1)
    row = lax.broadcasted_iota(jnp.int32, (k, lanes), 0)
    zero = jnp.zeros((k, lanes), jnp.float32)
    a_re = gram[:k]
    a_im = gram[k:]
    m_re = jnp.where(col == row, 1.0, zero)
    m_im = zero
    for j in range(k):
        at_col = col == j + off
        c_re = jnp.sum(jnp.where(at_col, a_re, 0.0), axis=1, keepdims=True)
        c_im = jnp.sum(jnp.where(at_col, a_im, 0.0), axis=1, keepdims=True)
        pivot = jnp.sqrt(c_re[j : j + 1])
        l_re = jnp.where(row[:, :1] > j, c_re / pivot, 0.0)
        l_im = jnp.where(row[:, :1] > j, c_im / pivot, 0.0)
        ar, ai = a_re[j : j + 1] / pivot, a_im[j : j + 1] / pivot
        mr, mi = m_re[j : j + 1] / pivot, m_im[j : j + 1] / pivot
        here = row == j
        a_re = jnp.where(here, ar, a_re - (l_re * ar - l_im * ai))
        a_im = jnp.where(here, ai, a_im - (l_re * ai + l_im * ar))
        m_re = jnp.where(here, mr, m_re - (l_re * mr - l_im * mi))
        m_im = jnp.where(here, mi, m_im - (l_re * mi + l_im * mr))
    return m_re, -m_im


def mix(m_re, m_im, rows, k):
    out_re = jnp.zeros((k, rows.shape[1]), jnp.float32)
    out_im = jnp.zeros((k, rows.shape[1]), jnp.float32)
    for j in range(k):
        f_re, f_im = m_re[:, j : j + 1], m_im[:, j : j + 1]
        r_re, r_im = rows[j : j + 1], rows[k + j : k + j + 1]
        out_re = out_re + (f_re * r_re - f_im * r_im)
        out_im = out_im + (f_re * r_im + f_im * r_re)
    return jnp.concatenate([out_re, out_im], axis=0)


def tn(left, right):
    return lax.dot_general(left, right, (((0,), (0,)), ((), ())), preferred_element_type=jnp.float32)


def fused_kernel(
    volts_ref, table_ref, start_ref, out_ref,
    stage, v_ref, z_ref, part_ref, land_ref, sum_ref, give_ref,
    f_send, f_recv, r_send, r_recv, g_send, g_recv, o_send, o_recv, own_sem,
    *, k, freq, tile, base, off,
):
    chans, _, spectra, width = v_ref.shape
    cols = volts_ref.shape[0]
    steps = spectra // STEP
    block = spectra // tile
    chunk = part_ref.shape[1] // tile
    group = lax.axis_index("freq")
    me = lax.axis_index("tile")
    barrier = pltpu.get_barrier_semaphore()
    for d in range(1, freq):
        pl.semaphore_signal(barrier, inc=1, device_id={"freq": lax.rem(group + d, freq)}, device_id_type=MESH)
    for d in range(1, tile):
        pl.semaphore_signal(barrier, inc=1, device_id={"tile": lax.rem(me + d, tile)}, device_id_type=MESH)
    pl.semaphore_wait(barrier, freq - 1 + tile - 1)

    span = (STEP + TAPS - 1) * P_SIZE
    my_cols = pl.ds(pl.multiple_of(group * cols, cols), cols)

    def handover(i, d):
        peer = lax.rem(group + d, freq)
        rows = pl.ds(pl.multiple_of(i * STEP, STEP), STEP)
        return pltpu.make_async_remote_copy(
            src_ref=stage.at[peer, :, :, rows, :],
            dst_ref=v_ref.at[:, :, rows, my_cols],
            send_sem=f_send.at[i, d - 1],
            recv_sem=f_recv.at[i, d - 1],
            device_id={"freq": peer},
            device_id_type=MESH,
        )

    def own_part(i):
        rows = pl.ds(pl.multiple_of(i * STEP, STEP), STEP)
        return pltpu.make_async_copy(
            stage.at[group, :, :, rows, :], v_ref.at[:, :, rows, my_cols], own_sem.at[i]
        )

    def filter_step(i, carry):
        start = pl.multiple_of(i * (STEP * P_SIZE), P_SIZE)
        result = nt(table_ref[...], volts_ref[:, pl.ds(start, span)])
        rows = pl.ds(pl.multiple_of(i * STEP, STEP), STEP)
        stage[:, :, :, rows, :] = result.reshape(freq, chans, 2, STEP, cols).astype(jnp.bfloat16)
        for d in range(1, freq):
            handover(i, d).start()
        own_part(i).start()
        return carry

    lax.fori_loop(0, steps, filter_step, 0)

    def filter_wait(i, carry):
        for d in range(1, freq):
            handover(i, d).wait()
        own_part(i).wait()
        return carry

    lax.fori_loop(0, steps, filter_wait, 0)

    mine = pl.ds(pl.multiple_of(me * chunk, 8), chunk)

    def tile_sum(at):
        sends = []
        for d in range(1, tile):
            peer = lax.rem(me + d, tile)
            copy = pltpu.make_async_remote_copy(
                src_ref=part_ref.at[at, pl.ds(pl.multiple_of(peer * chunk, 8), chunk)],
                dst_ref=land_ref.at[at, d - 1],
                send_sem=r_send.at[at, d - 1],
                recv_sem=r_recv.at[at, d - 1],
                device_id={"tile": peer},
                device_id_type=MESH,
            )
            copy.start()
            sends.append(copy)
        total = part_ref[at, mine]
        for d in range(1, tile):
            sends[d - 1].wait_recv()
            total = total + land_ref[at, d - 1]
        sum_ref[at, mine] = total
        for d in range(1, tile):
            copy = pltpu.make_async_remote_copy(
                src_ref=sum_ref.at[at, mine],
                dst_ref=sum_ref.at[at, mine],
                send_sem=g_send.at[at, d - 1],
                recv_sem=g_recv.at[at, d - 1],
                device_id={"tile": lax.rem(me + d, tile)},
                device_id_type=MESH,
            )
            copy.start()
            sends.append(copy)
        for copy in sends[tile - 1 :]:
            copy.wait_recv()
        return sends

    def rows_of(c):
        return slice(2 * k * c, 2 * k * (c + 1))

    part_ref[...] = jnp.zeros_like(part_ref)
    for c in range(chans):
        part_ref[0, rows_of(c), :spectra] = project(start_ref[...], v_ref[c, 0], v_ref[c, 1], k)
    pending = tile_sum(0)
    for step_at in range(ITERS):
        for c in range(chans):
            weights = sum_ref[step_at, rows_of(c), :spectra]
            if step_at == 0:
                basis = start_ref[...]
            else:
                m_re, m_im = inverse_factor(sum_ref[step_at, rows_of(c), base:], k, off)
                weights = mix(m_re, m_im, weights, k)
                basis = mix(m_re, m_im, z_ref[c], k)
            real_v, imag_v = v_ref[c, 0], v_ref[c, 1]
            parts = split3(weights / spectra)
            on_re = fold3(plain(parts, real_v))
            on_im = fold3(plain(parts, imag_v))
            z = jnp.concatenate([on_re[:k] - on_im[k:], on_re[k:] + on_im[:k]], axis=0) + loading * basis
            z_ref[c] = z
            before = [jnp.zeros((off, width), jnp.float32)] if off else []
            after = jnp.zeros((128 - off - k, width), jnp.float32)
            dims = (((1,), (1,)), ((), ()))
            on_zr, on_zi = [
                lax.dot_general(
                    z, jnp.concatenate(before + [half, after], axis=0), dims,
                    precision=highest, preferred_element_type=jnp.float32,
                )
                for half in (z[:k], z[k:])
            ]
            gram = jnp.concatenate([on_zr[:k] + on_zi[k:], on_zi[:k] - on_zr[k:]], axis=0)
            part_ref[step_at + 1, rows_of(c), base:] = gram
            part_ref[step_at + 1, rows_of(c), :spectra] = project(z, real_v, imag_v, k)
        pending += tile_sum(step_at + 1)

    n2 = 2 * k
    stride = tile * cols

    def give(c, d, f):
        peer = lax.rem(me + d, tile)
        lanes = pl.ds(pl.multiple_of(f * stride + me * cols, cols), cols)
        src = give_ref.at[peer, :, c, :, f * cols : (f + 1) * cols]
        dst = out_ref.at[:, c, :, lanes]
        if d == 0:
            return pltpu.make_async_copy(src, dst, own_sem.at[c * freq + f])
        return pltpu.make_async_remote_copy(
            src_ref=src,
            dst_ref=dst,
            send_sem=o_send.at[c, d - 1, f],
            recv_sem=o_recv.at[c, d - 1, f],
            device_id={"tile": peer},
            device_id_type=MESH,
        )

    copies = []
    for c in range(chans):
        m_re, m_im = inverse_factor(sum_ref[ITERS, rows_of(c), base:], k, off)
        w = mix(m_re, m_im, sum_ref[ITERS, rows_of(c), :spectra], k)
        q = mix(m_re, m_im, z_ref[c], k)
        turned = jnp.concatenate([q[k:], -q[:k]], axis=0)
        w3 = split3(w)
        w_left = jnp.concatenate([w3[:n2], w3[:n2], w3[n2 : 2 * n2], w3[n2 : 2 * n2], w3[:n2], w3[2 * n2 :]], axis=0)
        for r, side in ((0, q), (1, turned)):
            s3 = split3(side)
            s_right = jnp.concatenate(
                [s3[:n2], s3[n2 : 2 * n2], s3[:n2], s3[n2 : 2 * n2], s3[2 * n2 :], s3[:n2]], axis=0
            )
            cleaned = v_ref[c, r].astype(jnp.float32) - tn(w_left, s_right)
            give_ref[:, r, c] = cleaned.reshape(tile, block, width).astype(jnp.bfloat16)
        for d in range(tile):
            for f in range(freq):
                copy = give(c, d, f)
                copy.start()
                copies.append(copy)
    for copy in copies:
        copy.wait()
    for copy in pending:
        copy.wait_send()


def channelize_kernel(volts_ref, table_ref, out_ref):
    step = pl.program_id(0)
    span = (STEP + TAPS - 1) * P_SIZE
    start = pl.multiple_of(step * (STEP * P_SIZE), P_SIZE)
    chunk = volts_ref[:, pl.ds(start, span)]
    result = nt(table_ref[...], chunk)
    out_ref[...] = result.reshape(out_ref.shape).astype(jnp.bfloat16)


def channelize(voltages, table, rows, spectra_all):
    inputs_local, samples = voltages.shape
    return pl.pallas_call(
        channelize_kernel,
        grid=(spectra_all // STEP,),
        in_specs=[VMEM, VMEM],
        out_specs=pl.BlockSpec((rows, STEP, inputs_local), lambda i: (0, i, 0)),
        out_shape=jax.ShapeDtypeStruct((rows, spectra_all, inputs_local), jnp.bfloat16),
        compiler_params=pltpu.CompilerParams(vmem_limit_bytes=40 * 2**20),
    )(voltages, table)


def start_kernel(v_ref, q_ref, pg_ref, *, k, lanes):
    chans, _, spectra, _ = v_ref.shape
    pg_ref[...] = jnp.zeros_like(pg_ref)
    for c in range(chans):
        pg_ref[2 * k * c : 2 * k * (c + 1), :spectra] = project(q_ref[...], v_ref[c, 0], v_ref[c, 1], k)


def step_kernel(v_ref, z_ref, pg_ref, z_out, pg_out, *, k, lanes, first):
    chans, _, spectra, width = v_ref.shape
    pg_out[...] = jnp.zeros_like(pg_out)
    for c in range(chans):
        at = slice(2 * k * c, 2 * k * (c + 1))
        weights = pg_ref[at, :spectra]
        basis = z_ref[...] if first else z_ref[c]
        if not first:
            m_re, m_im = inverse_factor(pg_ref[at, lanes:], k)
            weights = mix(m_re, m_im, weights, k)
            basis = mix(m_re, m_im, basis, k)
        real_v, imag_v = v_ref[c, 0], v_ref[c, 1]
        parts = split3(weights / spectra)
        on_re = fold3(plain(parts, real_v))
        on_im = fold3(plain(parts, imag_v))
        z = jnp.concatenate([on_re[:k] - on_im[k:], on_re[k:] + on_im[:k]], axis=0) + loading * basis
        z_out[c] = z
        pg_out[at, :spectra] = project(z, real_v, imag_v, k)
        pad = jnp.zeros((lanes_pad(k), width), jnp.float32)
        right = jnp.concatenate([z[:k], pad], axis=0)
        right_im = jnp.concatenate([z[k:], pad], axis=0)
        dims = (((1,), (1,)), ((), ()))
        first_dot = lax.dot_general(z, right, dims, precision=highest, preferred_element_type=jnp.float32)
        second_dot = lax.dot_general(z, right_im, dims, precision=highest, preferred_element_type=jnp.float32)
        g_re = first_dot[:k] + second_dot[k:]
        g_im = second_dot[:k] - first_dot[k:]
        pg_out[at, lanes:] = jnp.concatenate([g_re, g_im], axis=0)


def lanes_pad(k):
    return 128 - k


def clean_kernel(v_ref, z_ref, pg_ref, out_ref, *, k, lanes):
    chans, _, spectra, width = v_ref.shape
    parts_count, _, _, block, _ = out_ref.shape
    for c in range(chans):
        at = slice(2 * k * c, 2 * k * (c + 1))
        m_re, m_im = inverse_factor(pg_ref[at, lanes:], k)
        w = mix(m_re, m_im, pg_ref[at, :spectra], k)
        q = mix(m_re, m_im, z_ref[c], k)
        turned = jnp.concatenate([q[k:], -q[:k]], axis=0)
        w3 = split3(w)
        n2 = 2 * k
        w_left = jnp.concatenate([w3[:n2], w3[:n2], w3[n2 : 2 * n2], w3[n2 : 2 * n2], w3[:n2], w3[2 * n2 :]], axis=0)
        for r, side in ((0, q), (1, turned)):
            s3 = split3(side)
            s_right = jnp.concatenate(
                [s3[:n2], s3[n2 : 2 * n2], s3[:n2], s3[n2 : 2 * n2], s3[2 * n2 :], s3[:n2]], axis=0
            )
            fitted = tn(w_left, s_right)
            cleaned = v_ref[c, r].astype(jnp.float32) - fitted
            out_ref[:, r, c] = cleaned.reshape(parts_count, block, width).astype(jnp.bfloat16)


def reduce_kernel(x_ref, out_ref, land_ref, send1, recv1, send2, recv2, *, size, chunk):
    me = lax.axis_index("tile")
    barrier = pltpu.get_barrier_semaphore()
    for d in range(1, size):
        peer = lax.rem(me + d, size)
        pl.semaphore_signal(barrier, inc=1, device_id={"tile": peer}, device_id_type=MESH)
    pl.semaphore_wait(barrier, size - 1)
    mine = pl.ds(pl.multiple_of(me * chunk, 8), chunk)
    sends = []
    for d in range(1, size):
        peer = lax.rem(me + d, size)
        copy = pltpu.make_async_remote_copy(
            src_ref=x_ref.at[pl.ds(pl.multiple_of(peer * chunk, 8), chunk)],
            dst_ref=land_ref.at[d - 1],
            send_sem=send1.at[d - 1],
            recv_sem=recv1.at[d - 1],
            device_id={"tile": peer},
            device_id_type=MESH,
        )
        copy.start()
        sends.append(copy)
    total = x_ref[mine]
    for d in range(1, size):
        sends[d - 1].wait_recv()
        total = total + land_ref[d - 1]
    out_ref[mine] = total
    later = []
    for d in range(1, size):
        peer = lax.rem(me + d, size)
        copy = pltpu.make_async_remote_copy(
            src_ref=out_ref.at[mine],
            dst_ref=out_ref.at[mine],
            send_sem=send2.at[d - 1],
            recv_sem=recv2.at[d - 1],
            device_id={"tile": peer},
            device_id_type=MESH,
        )
        copy.start()
        later.append(copy)
    for copy in later:
        copy.wait_recv()
    for copy in sends + later:
        copy.wait_send()


def tile_sum(x, size):
    rows, width = x.shape
    chunk = rows // size
    return pl.pallas_call(
        functools.partial(reduce_kernel, size=size, chunk=chunk),
        in_specs=[VMEM],
        out_specs=VMEM,
        out_shape=jax.ShapeDtypeStruct(x.shape, jnp.float32),
        scratch_shapes=[pltpu.VMEM((size - 1, chunk, width), jnp.float32)]
        + [pltpu.SemaphoreType.DMA((size - 1,))] * 4,
        compiler_params=pltpu.CompilerParams(collective_id=0, has_side_effects=True),
    )(x)


def up(value, unit):
    return -(-value // unit) * unit


def body_split(voltages, channel_ids, start_basis):
    inputs_local, samples_count = voltages.shape
    freq_count = lax.axis_size("freq")
    tile_count = lax.axis_size("tile")
    channels = channel_ids.shape[0]
    chan_local = channels // freq_count
    spectra_all = samples_count // P_SIZE - TAPS + 1
    spectra_local = spectra_all // tile_count
    k = start_basis.shape[1]
    width = freq_count * inputs_local

    coeffs = make_table(channel_ids, TAPS, P_SIZE).reshape(TAPS, 2 * channels, P_SIZE)
    local = channelize(voltages, banded(coeffs), 2 * channels, spectra_all)
    parcel = local.reshape(2, freq_count, chan_local, spectra_all, inputs_local)
    arrived = lax.all_to_all(parcel, "freq", split_axis=1, concat_axis=1, tiled=True)
    values = jnp.transpose(arrived, (2, 0, 3, 1, 4)).reshape(chan_local, 2, spectra_all, width)

    mine = lax.axis_index("tile")
    start = start_basis.reshape(2 * k, freq_count, tile_count, inputs_local)
    start = lax.dynamic_index_in_dim(start, mine, 2, keepdims=False).reshape(2 * k, width)

    lanes = up(spectra_all, 128)
    chunk = up(-(-chan_local * 2 * k // tile_count), 8)
    packed = jax.ShapeDtypeStruct((tile_count * chunk, lanes + 128), jnp.float32)
    z_shape = jax.ShapeDtypeStruct((chan_local, 2 * k, width), jnp.float32)
    params = pltpu.CompilerParams(vmem_limit_bytes=40 * 2**20)

    partial = pl.pallas_call(
        functools.partial(start_kernel, k=k, lanes=lanes),
        in_specs=[VMEM] * 2, out_specs=VMEM, out_shape=packed, compiler_params=params,
    )(values, start)
    z = start
    for step_at in range(ITERS):
        total = tile_sum(partial, tile_count)
        z, partial = pl.pallas_call(
            functools.partial(step_kernel, k=k, lanes=lanes, first=step_at == 0),
            in_specs=[VMEM] * 3, out_specs=[VMEM] * 2, out_shape=[z_shape, packed],
            compiler_params=params,
        )(values, z, total)
    total = tile_sum(partial, tile_count)
    cleaned = pl.pallas_call(
        functools.partial(clean_kernel, k=k, lanes=lanes),
        in_specs=[VMEM] * 3, out_specs=VMEM,
        out_shape=jax.ShapeDtypeStruct((tile_count, 2, chan_local, spectra_local, width), jnp.bfloat16),
        compiler_params=params,
    )(values, z, total)
    moved = lax.all_to_all(cleaned, "tile", split_axis=0, concat_axis=0, tiled=True)
    moved = moved.reshape(tile_count, 2, chan_local, spectra_local, freq_count, inputs_local)
    moved = jnp.transpose(moved, (1, 2, 3, 4, 0, 5)).astype(jnp.float32)
    return moved.reshape(2, chan_local, spectra_local, freq_count * tile_count * inputs_local)


def body(voltages, channel_ids, start_basis):
    inputs_local, samples_count = voltages.shape
    freq_count = lax.axis_size("freq")
    tile_count = lax.axis_size("tile")
    if inputs_local % 128:
        return body_split(voltages, channel_ids, start_basis)
    channels = channel_ids.shape[0]
    chan_local = channels // freq_count
    spectra_all = samples_count // P_SIZE - TAPS + 1
    spectra_local = spectra_all // tile_count
    k = start_basis.shape[1]
    width = freq_count * inputs_local

    coeffs = make_table(channel_ids, TAPS, P_SIZE)
    coeffs = coeffs.reshape(TAPS, 2, channels, P_SIZE).transpose(0, 2, 1, 3).reshape(TAPS, 2 * channels, P_SIZE)
    mine = lax.axis_index("tile")
    start = start_basis.reshape(2 * k, freq_count, tile_count, inputs_local)
    start = lax.dynamic_index_in_dim(start, mine, 2, keepdims=False).reshape(2 * k, width)

    base, off = spectra_all // 128 * 128, spectra_all % 128
    if off + k > 128:
        base, off = base + 128, 0
    rows = tile_count * up(-(-chan_local * 2 * k // tile_count), 8)
    chunk = rows // tile_count
    rounds = ITERS + 1
    peers = tile_count - 1
    steps = spectra_all // STEP
    sem = pltpu.SemaphoreType.DMA
    cleaned = pl.pallas_call(
        functools.partial(fused_kernel, k=k, freq=freq_count, tile=tile_count, base=base, off=off),
        in_specs=[VMEM] * 3,
        out_specs=VMEM,
        out_shape=jax.ShapeDtypeStruct(
            (2, chan_local, spectra_local, width * tile_count), jnp.bfloat16
        ),
        scratch_shapes=[
            pltpu.VMEM((freq_count, chan_local, 2, spectra_all, inputs_local), jnp.bfloat16),
            pltpu.VMEM((chan_local, 2, spectra_all, width), jnp.bfloat16),
            pltpu.VMEM((chan_local, 2 * k, width), jnp.float32),
            pltpu.VMEM((rounds, rows, base + 128), jnp.float32),
            pltpu.VMEM((rounds, peers, chunk, base + 128), jnp.float32),
            pltpu.VMEM((rounds, rows, base + 128), jnp.float32),
            pltpu.VMEM((tile_count, 2, chan_local, spectra_local, width), jnp.bfloat16),
            sem((steps, freq_count - 1)), sem((steps, freq_count - 1)),
            sem((rounds, peers)), sem((rounds, peers)),
            sem((rounds, peers)), sem((rounds, peers)),
            sem((chan_local, peers, freq_count)), sem((chan_local, peers, freq_count)),
            sem((max(steps, chan_local * freq_count),)),
        ],
        compiler_params=pltpu.CompilerParams(
            collective_id=0, has_side_effects=True, vmem_limit_bytes=56 * 2**20
        ),
    )(voltages, banded(coeffs), start)
    return cleaned.astype(jnp.float32)


def solution(mesh):
    in_specs = (P(("freq", "tile"), None), P(), P())
    out_specs = P(None, "freq", "tile", None)
    return jax.shard_map(body, mesh=mesh, in_specs=in_specs, out_specs=out_specs, check_vma=False)
```

```python
import functools
import math

import jax
import jax.numpy as jnp
from jax import lax
from jax.experimental import pallas as pl
from jax.experimental.pallas import tpu as pltpu
from jax.sharding import PartitionSpec as P

TAPS = 4
P_SIZE = 128
ITERS = 3
STEP = 16

loading = 0.5
highest = lax.Precision.HIGHEST
VMEM = pl.BlockSpec(memory_space=pltpu.VMEM)
MESH = pl.DeviceIdType.MESH


def make_table(channel_ids, taps_count, points):
    length = taps_count * points
    offsets = jnp.arange(length, dtype=jnp.float32)
    shifted = (offsets + 0.5 - length / 2.0) / points
    window = jnp.sinc(shifted) * (0.5 - 0.5 * jnp.cos(2.0 * math.pi * (offsets + 0.5) / length))
    window = window / jnp.sqrt(jnp.sum(window * window))
    window = window.reshape(taps_count, points)
    phases = channel_ids[:, None] * jnp.arange(points, dtype=jnp.int32)[None, :] % points
    angles = 2.0 * math.pi / points * phases.astype(jnp.float32)
    rotors = jnp.stack([jnp.cos(angles), -jnp.sin(angles)])
    return (window[:, None, None, :] * rotors[None]).astype(jnp.bfloat16)


def banded(coeffs):
    rows = coeffs.shape[1]
    spect = lax.broadcasted_iota(jnp.int32, (1, STEP, STEP + TAPS - 1, 1), 1)
    frame = lax.broadcasted_iota(jnp.int32, (1, STEP, STEP + TAPS - 1, 1), 2)
    table = jnp.zeros((rows, STEP, STEP + TAPS - 1, P_SIZE), jnp.bfloat16)
    for tap in range(TAPS):
        table = jnp.where(frame - spect == tap, coeffs[tap][:, None, None, :], table)
    return table.reshape(rows * STEP, (STEP + TAPS - 1) * P_SIZE)


def banded_frames(coeffs):
    rows = coeffs.shape[1]
    shape = (STEP + TAPS - 1, 1, STEP, 1)
    lag = lax.broadcasted_iota(jnp.int32, shape, 0) - lax.broadcasted_iota(jnp.int32, shape, 2)
    table = jnp.zeros((STEP + TAPS - 1, rows, STEP, P_SIZE), jnp.bfloat16)
    for tap in range(TAPS):
        table = jnp.where(lag == tap, coeffs[tap][None, :, None, :], table)
    return table.reshape(STEP + TAPS - 1, rows * STEP, P_SIZE)


def nt(left, right):
    return lax.dot_general(left, right, (((1,), (1,)), ((), ())), preferred_element_type=jnp.float32)


def split3(value):
    high = value.astype(jnp.bfloat16)
    rest = value - high.astype(jnp.float32)
    mid = rest.astype(jnp.bfloat16)
    low = (rest - mid.astype(jnp.float32)).astype(jnp.bfloat16)
    return jnp.concatenate([high, mid, low], axis=0)


def fold3(value):
    rows = value.shape[0] // 3
    return value[:rows] + value[rows : 2 * rows] + value[2 * rows :]


def plain(left, right):
    return lax.dot_general(left, right, (((1,), (0,)), ((), ())), preferred_element_type=jnp.float32)


def project(z, real_v, imag_v, k):
    parts = split3(z)
    on_re = fold3(nt(parts, real_v))
    on_im = fold3(nt(parts, imag_v))
    return jnp.concatenate([on_re[:k] + on_im[k:], on_re[k:] - on_im[:k]], axis=0)


def inverse_factor(gram, k, off=0):
    lanes = gram.shape[1]
    col = lax.broadcasted_iota(jnp.int32, (k, lanes), 1)
    row = lax.broadcasted_iota(jnp.int32, (k, lanes), 0)
    zero = jnp.zeros((k, lanes), jnp.float32)
    a_re = gram[:k]
    a_im = gram[k:]
    m_re = jnp.where(col == row, 1.0, zero)
    m_im = zero
    for j in range(k):
        at_col = col == j + off
        c_re = jnp.sum(jnp.where(at_col, a_re, 0.0), axis=1, keepdims=True)
        c_im = jnp.sum(jnp.where(at_col, a_im, 0.0), axis=1, keepdims=True)
        pivot = jnp.sqrt(c_re[j : j + 1])
        l_re = jnp.where(row[:, :1] > j, c_re / pivot, 0.0)
        l_im = jnp.where(row[:, :1] > j, c_im / pivot, 0.0)
        ar, ai = a_re[j : j + 1] / pivot, a_im[j : j + 1] / pivot
        mr, mi = m_re[j : j + 1] / pivot, m_im[j : j + 1] / pivot
        here = row == j
        a_re = jnp.where(here, ar, a_re - (l_re * ar - l_im * ai))
        a_im = jnp.where(here, ai, a_im - (l_re * ai + l_im * ar))
        m_re = jnp.where(here, mr, m_re - (l_re * mr - l_im * mi))
        m_im = jnp.where(here, mi, m_im - (l_re * mi + l_im * mr))
    return m_re, -m_im


def mix(m_re, m_im, rows, k):
    out_re = jnp.zeros((k, rows.shape[1]), jnp.float32)
    out_im = jnp.zeros((k, rows.shape[1]), jnp.float32)
    for j in range(k):
        f_re, f_im = m_re[:, j : j + 1], m_im[:, j : j + 1]
        r_re, r_im = rows[j : j + 1], rows[k + j : k + j + 1]
        out_re = out_re + (f_re * r_re - f_im * r_im)
        out_im = out_im + (f_re * r_im + f_im * r_re)
    return jnp.concatenate([out_re, out_im], axis=0)


def tn(left, right):
    return lax.dot_general(left, right, (((0,), (0,)), ((), ())), preferred_element_type=jnp.float32)


def fused_kernel(
    volts_ref, table_ref, start_ref, out_ref,
    stage, v_ref, z_ref, part_ref, land_ref, sum_ref, give_ref,
    volts_vmem, volts_sem, f_send, f_recv, r_send, r_recv, g_send, g_recv, o_send, o_recv, own_sem,
    *, k, freq, tile, base, off,
):
    chans, _, spectra, width = v_ref.shape
    cols = volts_ref.shape[0]
    steps = spectra // STEP
    block = spectra // tile
    chunk = part_ref.shape[1] // tile
    group = lax.axis_index("freq")
    me = lax.axis_index("tile")
    barrier = pltpu.get_barrier_semaphore()
    for d in range(1, freq):
        pl.semaphore_signal(barrier, inc=1, device_id={"freq": lax.rem(group + d, freq)}, device_id_type=MESH)
    for d in range(1, tile):
        pl.semaphore_signal(barrier, inc=1, device_id={"tile": lax.rem(me + d, tile)}, device_id_type=MESH)
    lead = (TAPS - 1) * P_SIZE

    def fetch(i):
        at = pl.ds(pl.multiple_of(lead + i * (STEP * P_SIZE), P_SIZE), STEP * P_SIZE)
        return pltpu.make_async_copy(volts_ref.at[:, at], volts_vmem.at[:, at], volts_sem.at[i])

    head = pltpu.make_async_copy(
        volts_ref.at[:, :lead], volts_vmem.at[:, :lead], volts_sem.at[steps]
    )
    head.start()

    def fetch_start(i, carry):
        fetch(i).start()
        return carry

    lax.fori_loop(0, steps, fetch_start, 0)
    pl.semaphore_wait(barrier, freq - 1 + tile - 1)
    head.wait()

    span = (STEP + TAPS - 1) * P_SIZE
    my_cols = pl.ds(pl.multiple_of(group * cols, cols), cols)

    def handover(i, d):
        peer = lax.rem(group + d, freq)
        rows = pl.ds(pl.multiple_of(i * STEP, STEP), STEP)
        return pltpu.make_async_remote_copy(
            src_ref=stage.at[peer, :, :, rows, :],
            dst_ref=v_ref.at[:, :, rows, my_cols],
            send_sem=f_send.at[i, d - 1],
            recv_sem=f_recv.at[i, d - 1],
            device_id={"freq": peer},
            device_id_type=MESH,
        )

    def own_part(i):
        rows = pl.ds(pl.multiple_of(i * STEP, STEP), STEP)
        return pltpu.make_async_copy(
            stage.at[group, :, :, rows, :], v_ref.at[:, :, rows, my_cols], own_sem.at[i]
        )

    def filter_step(i, carry):
        start = pl.multiple_of(i * (STEP * P_SIZE), P_SIZE)
        fetch(i).wait()
        table = jnp.concatenate([table_ref[at] for at in range(STEP + TAPS - 1)], axis=1)
        result = nt(table, volts_vmem[:, pl.ds(start, span)])
        rows = pl.ds(pl.multiple_of(i * STEP, STEP), STEP)
        stage[:, :, :, rows, :] = result.reshape(freq, chans, 2, STEP, cols).astype(jnp.bfloat16)
        for d in range(1, freq):
            handover(i, d).start()
        own_part(i).start()
        return carry

    lax.fori_loop(0, steps, filter_step, 0)

    def filter_wait(i, carry):
        for d in range(1, freq):
            handover(i, d).wait()
        own_part(i).wait()
        return carry

    lax.fori_loop(0, steps, filter_wait, 0)

    mine = pl.ds(pl.multiple_of(me * chunk, 8), chunk)

    def tile_sum(at):
        sends = []
        for d in range(1, tile):
            peer = lax.rem(me + d, tile)
            copy = pltpu.make_async_remote_copy(
                src_ref=part_ref.at[at, pl.ds(pl.multiple_of(peer * chunk, 8), chunk)],
                dst_ref=land_ref.at[at, d - 1],
                send_sem=r_send.at[at, d - 1],
                recv_sem=r_recv.at[at, d - 1],
                device_id={"tile": peer},
                device_id_type=MESH,
            )
            copy.start()
            sends.append(copy)
        total = part_ref[at, mine]
        for d in range(1, tile):
            sends[d - 1].wait_recv()
            total = total + land_ref[at, d - 1]
        sum_ref[at, mine] = total
        for d in range(1, tile):
            copy = pltpu.make_async_remote_copy(
                src_ref=sum_ref.at[at, mine],
                dst_ref=sum_ref.at[at, mine],
                send_sem=g_send.at[at, d - 1],
                recv_sem=g_recv.at[at, d - 1],
                device_id={"tile": lax.rem(me + d, tile)},
                device_id_type=MESH,
            )
            copy.start()
            sends.append(copy)
        for copy in sends[tile - 1 :]:
            copy.wait_recv()
        return sends

    def rows_of(c):
        return slice(2 * k * c, 2 * k * (c + 1))

    part_ref[...] = jnp.zeros_like(part_ref)
    for c in range(chans):
        part_ref[0, rows_of(c), :spectra] = project(start_ref[...], v_ref[c, 0], v_ref[c, 1], k)
    pending = tile_sum(0)
    for step_at in range(ITERS):
        for c in range(chans):
            weights = sum_ref[step_at, rows_of(c), :spectra]
            if step_at == 0:
                basis = start_ref[...]
            else:
                m_re, m_im = inverse_factor(sum_ref[step_at, rows_of(c), base:], k, off)
                weights = mix(m_re, m_im, weights, k)
                basis = mix(m_re, m_im, z_ref[c], k)
            real_v, imag_v = v_ref[c, 0], v_ref[c, 1]
            parts = split3(weights / spectra)
            on_re = fold3(plain(parts, real_v))
            on_im = fold3(plain(parts, imag_v))
            z = jnp.concatenate([on_re[:k] - on_im[k:], on_re[k:] + on_im[:k]], axis=0) + loading * basis
            z_ref[c] = z
            before = [jnp.zeros((off, width), jnp.float32)] if off else []
            after = jnp.zeros((128 - off - k, width), jnp.float32)
            dims = (((1,), (1,)), ((), ()))
            on_zr, on_zi = [
                lax.dot_general(
                    z, jnp.concatenate(before + [half, after], axis=0), dims,
                    precision=highest, preferred_element_type=jnp.float32,
                )
                for half in (z[:k], z[k:])
            ]
            gram = jnp.concatenate([on_zr[:k] + on_zi[k:], on_zi[:k] - on_zr[k:]], axis=0)
            part_ref[step_at + 1, rows_of(c), base:] = gram
            part_ref[step_at + 1, rows_of(c), :spectra] = project(z, real_v, imag_v, k)
        pending += tile_sum(step_at + 1)

    n2 = 2 * k
    stride = tile * cols

    def give(c, d, f):
        peer = lax.rem(me + d, tile)
        lanes = pl.ds(pl.multiple_of(f * stride + me * cols, cols), cols)
        src = give_ref.at[peer, :, c, :, f * cols : (f + 1) * cols]
        dst = out_ref.at[:, c, :, lanes]
        if d == 0:
            return pltpu.make_async_copy(src, dst, own_sem.at[c * freq + f])
        return pltpu.make_async_remote_copy(
            src_ref=src,
            dst_ref=dst,
            send_sem=o_send.at[c, d - 1, f],
            recv_sem=o_recv.at[c, d - 1, f],
            device_id={"tile": peer},
            device_id_type=MESH,
        )

    copies = []
    for c in range(chans):
        m_re, m_im = inverse_factor(sum_ref[ITERS, rows_of(c), base:], k, off)
        w = mix(m_re, m_im, sum_ref[ITERS, rows_of(c), :spectra], k)
        q = mix(m_re, m_im, z_ref[c], k)
        turned = jnp.concatenate([q[k:], -q[:k]], axis=0)
        w3 = split3(w)
        w_left = jnp.concatenate([w3[:n2], w3[:n2], w3[n2 : 2 * n2], w3[n2 : 2 * n2], w3[:n2], w3[2 * n2 :]], axis=0)
        for r, side in ((0, q), (1, turned)):
            s3 = split3(side)
            s_right = jnp.concatenate(
                [s3[:n2], s3[n2 : 2 * n2], s3[:n2], s3[n2 : 2 * n2], s3[2 * n2 :], s3[:n2]], axis=0
            )
            cleaned = v_ref[c, r].astype(jnp.float32) - tn(w_left, s_right)
            give_ref[:, r, c] = cleaned.reshape(tile, block, width).astype(jnp.bfloat16)
        for d in range(tile):
            for f in range(freq):
                copy = give(c, d, f)
                copy.start()
                copies.append(copy)
    for copy in copies:
        copy.wait()
    for copy in pending:
        copy.wait_send()


def channelize_kernel(volts_ref, table_ref, out_ref):
    step = pl.program_id(0)
    span = (STEP + TAPS - 1) * P_SIZE
    start = pl.multiple_of(step * (STEP * P_SIZE), P_SIZE)
    chunk = volts_ref[:, pl.ds(start, span)]
    result = nt(table_ref[...], chunk)
    out_ref[...] = result.reshape(out_ref.shape).astype(jnp.bfloat16)


def channelize(voltages, table, rows, spectra_all):
    inputs_local, samples = voltages.shape
    return pl.pallas_call(
        channelize_kernel,
        grid=(spectra_all // STEP,),
        in_specs=[VMEM, VMEM],
        out_specs=pl.BlockSpec((rows, STEP, inputs_local), lambda i: (0, i, 0)),
        out_shape=jax.ShapeDtypeStruct((rows, spectra_all, inputs_local), jnp.bfloat16),
        compiler_params=pltpu.CompilerParams(vmem_limit_bytes=40 * 2**20),
    )(voltages, table)


def start_kernel(v_ref, q_ref, pg_ref, *, k, lanes):
    chans, _, spectra, _ = v_ref.shape
    pg_ref[...] = jnp.zeros_like(pg_ref)
    for c in range(chans):
        pg_ref[2 * k * c : 2 * k * (c + 1), :spectra] = project(q_ref[...], v_ref[c, 0], v_ref[c, 1], k)


def step_kernel(v_ref, z_ref, pg_ref, z_out, pg_out, *, k, lanes, first):
    chans, _, spectra, width = v_ref.shape
    pg_out[...] = jnp.zeros_like(pg_out)
    for c in range(chans):
        at = slice(2 * k * c, 2 * k * (c + 1))
        weights = pg_ref[at, :spectra]
        basis = z_ref[...] if first else z_ref[c]
        if not first:
            m_re, m_im = inverse_factor(pg_ref[at, lanes:], k)
            weights = mix(m_re, m_im, weights, k)
            basis = mix(m_re, m_im, basis, k)
        real_v, imag_v = v_ref[c, 0], v_ref[c, 1]
        parts = split3(weights / spectra)
        on_re = fold3(plain(parts, real_v))
        on_im = fold3(plain(parts, imag_v))
        z = jnp.concatenate([on_re[:k] - on_im[k:], on_re[k:] + on_im[:k]], axis=0) + loading * basis
        z_out[c] = z
        pg_out[at, :spectra] = project(z, real_v, imag_v, k)
        pad = jnp.zeros((lanes_pad(k), width), jnp.float32)
        right = jnp.concatenate([z[:k], pad], axis=0)
        right_im = jnp.concatenate([z[k:], pad], axis=0)
        dims = (((1,), (1,)), ((), ()))
        first_dot = lax.dot_general(z, right, dims, precision=highest, preferred_element_type=jnp.float32)
        second_dot = lax.dot_general(z, right_im, dims, precision=highest, preferred_element_type=jnp.float32)
        g_re = first_dot[:k] + second_dot[k:]
        g_im = second_dot[:k] - first_dot[k:]
        pg_out[at, lanes:] = jnp.concatenate([g_re, g_im], axis=0)


def lanes_pad(k):
    return 128 - k


def clean_kernel(v_ref, z_ref, pg_ref, out_ref, *, k, lanes):
    chans, _, spectra, width = v_ref.shape
    parts_count, _, _, block, _ = out_ref.shape
    for c in range(chans):
        at = slice(2 * k * c, 2 * k * (c + 1))
        m_re, m_im = inverse_factor(pg_ref[at, lanes:], k)
        w = mix(m_re, m_im, pg_ref[at, :spectra], k)
        q = mix(m_re, m_im, z_ref[c], k)
        turned = jnp.concatenate([q[k:], -q[:k]], axis=0)
        w3 = split3(w)
        n2 = 2 * k
        w_left = jnp.concatenate([w3[:n2], w3[:n2], w3[n2 : 2 * n2], w3[n2 : 2 * n2], w3[:n2], w3[2 * n2 :]], axis=0)
        for r, side in ((0, q), (1, turned)):
            s3 = split3(side)
            s_right = jnp.concatenate(
                [s3[:n2], s3[n2 : 2 * n2], s3[:n2], s3[n2 : 2 * n2], s3[2 * n2 :], s3[:n2]], axis=0
            )
            fitted = tn(w_left, s_right)
            cleaned = v_ref[c, r].astype(jnp.float32) - fitted
            out_ref[:, r, c] = cleaned.reshape(parts_count, block, width).astype(jnp.bfloat16)


def reduce_kernel(x_ref, out_ref, land_ref, send1, recv1, send2, recv2, *, size, chunk):
    me = lax.axis_index("tile")
    barrier = pltpu.get_barrier_semaphore()
    for d in range(1, size):
        peer = lax.rem(me + d, size)
        pl.semaphore_signal(barrier, inc=1, device_id={"tile": peer}, device_id_type=MESH)
    pl.semaphore_wait(barrier, size - 1)
    mine = pl.ds(pl.multiple_of(me * chunk, 8), chunk)
    sends = []
    for d in range(1, size):
        peer = lax.rem(me + d, size)
        copy = pltpu.make_async_remote_copy(
            src_ref=x_ref.at[pl.ds(pl.multiple_of(peer * chunk, 8), chunk)],
            dst_ref=land_ref.at[d - 1],
            send_sem=send1.at[d - 1],
            recv_sem=recv1.at[d - 1],
            device_id={"tile": peer},
            device_id_type=MESH,
        )
        copy.start()
        sends.append(copy)
    total = x_ref[mine]
    for d in range(1, size):
        sends[d - 1].wait_recv()
        total = total + land_ref[d - 1]
    out_ref[mine] = total
    later = []
    for d in range(1, size):
        peer = lax.rem(me + d, size)
        copy = pltpu.make_async_remote_copy(
            src_ref=out_ref.at[mine],
            dst_ref=out_ref.at[mine],
            send_sem=send2.at[d - 1],
            recv_sem=recv2.at[d - 1],
            device_id={"tile": peer},
            device_id_type=MESH,
        )
        copy.start()
        later.append(copy)
    for copy in later:
        copy.wait_recv()
    for copy in sends + later:
        copy.wait_send()


def tile_sum(x, size):
    rows, width = x.shape
    chunk = rows // size
    return pl.pallas_call(
        functools.partial(reduce_kernel, size=size, chunk=chunk),
        in_specs=[VMEM],
        out_specs=VMEM,
        out_shape=jax.ShapeDtypeStruct(x.shape, jnp.float32),
        scratch_shapes=[pltpu.VMEM((size - 1, chunk, width), jnp.float32)]
        + [pltpu.SemaphoreType.DMA((size - 1,))] * 4,
        compiler_params=pltpu.CompilerParams(collective_id=0, has_side_effects=True),
    )(x)


def up(value, unit):
    return -(-value // unit) * unit


def body_split(voltages, channel_ids, start_basis):
    inputs_local, samples_count = voltages.shape
    freq_count = lax.axis_size("freq")
    tile_count = lax.axis_size("tile")
    channels = channel_ids.shape[0]
    chan_local = channels // freq_count
    spectra_all = samples_count // P_SIZE - TAPS + 1
    spectra_local = spectra_all // tile_count
    k = start_basis.shape[1]
    width = freq_count * inputs_local

    coeffs = make_table(channel_ids, TAPS, P_SIZE).reshape(TAPS, 2 * channels, P_SIZE)
    local = channelize(voltages, banded(coeffs), 2 * channels, spectra_all)
    parcel = local.reshape(2, freq_count, chan_local, spectra_all, inputs_local)
    arrived = lax.all_to_all(parcel, "freq", split_axis=1, concat_axis=1, tiled=True)
    values = jnp.transpose(arrived, (2, 0, 3, 1, 4)).reshape(chan_local, 2, spectra_all, width)

    mine = lax.axis_index("tile")
    start = start_basis.reshape(2 * k, freq_count, tile_count, inputs_local)
    start = lax.dynamic_index_in_dim(start, mine, 2, keepdims=False).reshape(2 * k, width)

    lanes = up(spectra_all, 128)
    chunk = up(-(-chan_local * 2 * k // tile_count), 8)
    packed = jax.ShapeDtypeStruct((tile_count * chunk, lanes + 128), jnp.float32)
    z_shape = jax.ShapeDtypeStruct((chan_local, 2 * k, width), jnp.float32)
    params = pltpu.CompilerParams(vmem_limit_bytes=40 * 2**20)

    partial = pl.pallas_call(
        functools.partial(start_kernel, k=k, lanes=lanes),
        in_specs=[VMEM] * 2, out_specs=VMEM, out_shape=packed, compiler_params=params,
    )(values, start)
    z = start
    for step_at in range(ITERS):
        total = tile_sum(partial, tile_count)
        z, partial = pl.pallas_call(
            functools.partial(step_kernel, k=k, lanes=lanes, first=step_at == 0),
            in_specs=[VMEM] * 3, out_specs=[VMEM] * 2, out_shape=[z_shape, packed],
            compiler_params=params,
        )(values, z, total)
    total = tile_sum(partial, tile_count)
    cleaned = pl.pallas_call(
        functools.partial(clean_kernel, k=k, lanes=lanes),
        in_specs=[VMEM] * 3, out_specs=VMEM,
        out_shape=jax.ShapeDtypeStruct((tile_count, 2, chan_local, spectra_local, width), jnp.bfloat16),
        compiler_params=params,
    )(values, z, total)
    moved = lax.all_to_all(cleaned, "tile", split_axis=0, concat_axis=0, tiled=True)
    moved = moved.reshape(tile_count, 2, chan_local, spectra_local, freq_count, inputs_local)
    moved = jnp.transpose(moved, (1, 2, 3, 4, 0, 5)).astype(jnp.float32)
    return moved.reshape(2, chan_local, spectra_local, freq_count * tile_count * inputs_local)


def body(voltages, channel_ids, start_basis):
    inputs_local, samples_count = voltages.shape
    freq_count = lax.axis_size("freq")
    tile_count = lax.axis_size("tile")
    if inputs_local % 128:
        return body_split(voltages, channel_ids, start_basis)
    channels = channel_ids.shape[0]
    chan_local = channels // freq_count
    spectra_all = samples_count // P_SIZE - TAPS + 1
    spectra_local = spectra_all // tile_count
    k = start_basis.shape[1]
    width = freq_count * inputs_local

    coeffs = make_table(channel_ids, TAPS, P_SIZE)
    coeffs = coeffs.reshape(TAPS, 2, channels, P_SIZE).transpose(0, 2, 1, 3).reshape(TAPS, 2 * channels, P_SIZE)
    mine = lax.axis_index("tile")
    start = start_basis.reshape(2 * k, freq_count, tile_count, inputs_local)
    start = lax.dynamic_index_in_dim(start, mine, 2, keepdims=False).reshape(2 * k, width)

    base, off = spectra_all // 128 * 128, spectra_all % 128
    if off + k > 128:
        base, off = base + 128, 0
    rows = tile_count * up(-(-chan_local * 2 * k // tile_count), 8)
    chunk = rows // tile_count
    rounds = ITERS + 1
    peers = tile_count - 1
    steps = spectra_all // STEP
    sem = pltpu.SemaphoreType.DMA
    cleaned = pl.pallas_call(
        functools.partial(fused_kernel, k=k, freq=freq_count, tile=tile_count, base=base, off=off),
        in_specs=[pl.BlockSpec(memory_space=pl.ANY), VMEM, VMEM],
        out_specs=VMEM,
        out_shape=jax.ShapeDtypeStruct(
            (2, chan_local, spectra_local, width * tile_count), jnp.bfloat16
        ),
        scratch_shapes=[
            pltpu.VMEM((freq_count, chan_local, 2, spectra_all, inputs_local), jnp.bfloat16),
            pltpu.VMEM((chan_local, 2, spectra_all, width), jnp.bfloat16),
            pltpu.VMEM((chan_local, 2 * k, width), jnp.float32),
            pltpu.VMEM((rounds, rows, base + 128), jnp.float32),
            pltpu.VMEM((rounds, peers, chunk, base + 128), jnp.float32),
            pltpu.VMEM((rounds, rows, base + 128), jnp.float32),
            pltpu.VMEM((tile_count, 2, chan_local, spectra_local, width), jnp.bfloat16),
            pltpu.VMEM((inputs_local, samples_count), jnp.bfloat16),
            sem((steps + 1,)),
            sem((steps, freq_count - 1)), sem((steps, freq_count - 1)),
            sem((rounds, peers)), sem((rounds, peers)),
            sem((rounds, peers)), sem((rounds, peers)),
            sem((chan_local, peers, freq_count)), sem((chan_local, peers, freq_count)),
            sem((max(steps, chan_local * freq_count),)),
        ],
        compiler_params=pltpu.CompilerParams(
            collective_id=0, has_side_effects=True, vmem_limit_bytes=56 * 2**20
        ),
    )(voltages, banded_frames(coeffs), start)
    return cleaned.astype(jnp.float32)


def solution(mesh):
    in_specs = (P(("freq", "tile"), None), P(), P())
    out_specs = P(None, "freq", "tile", None)
    return jax.shard_map(body, mesh=mesh, in_specs=in_specs, out_specs=out_specs, check_vma=False)
```
